32 devices in a mesh: vec: 4 (over y, x), walk: 8 (over z, core).
Axes of the slice: x: 2, y: 2, z: 4, core: 2. Of those that a mesh axis runs over, the one named last changes fastest.
Arguments:
- walkers: bfloat16 [128, 1024, 128], P('walk', 'vec'), may hold values from -6 to 6
- inverse: bfloat16 [128, 2, 2, 32, 32], P('walk'), may hold values from -0.75 to 0.75
- vectors: bfloat16 [10240, 1024, 128], P('walk', 'vec'), may hold values from -0.015625 to 0.015625
- sources: int32 [128], replicated, may hold values from 0 to 127
Outputs:
- moved: bfloat16 [128, 1024, 128], P('walk', 'vec')
- force_bias: float32 [2, 128, 10240], P(None, 'vec', 'walk')
The draws below stay inside these ranges and needn't reach their ends.
Inputs may be any that keep to these rules, and one draw needn't show every extreme that they name: New walker j is a copy of old walker sources[j]; an old walker may be copied many times or not at all.
All inputs are finite; a program needn't handle non-finite values.
Results may differ from the reference program's by a relative error of at most 0.0029.
Values may be sent and summed in bfloat16 or wider, within the bound.
A program may use at most 256 MiB of HBM per device.

```python
import math
import jax
import jax.numpy as jnp
import numpy as np
from jax import lax

M = 1024
NOCC = 32
NCHOL = 10240
W = 128


def set_ends(array, key, smallest, top_value):
    index_at = [jax.random.randint(jax.random.fold_in(key, axis), (), 0, length) for axis, length in enumerate(array.shape)]
    widest = array.shape.index(max(array.shape))
    next_to = index_at[:widest] + [(index_at[widest] + 1) % array.shape[widest]] + index_at[widest + 1:]
    return array.at[tuple(index_at)].set(smallest).at[tuple(next_to)].set(top_value)


def shard_levels(stream_key, shape, shards, smallest, largest):
    factor_of, own = 1.0, jax.random.fold_in(stream_key, 6)
    for position, blocks in shards:
        heights = jnp.exp(jax.random.uniform(jax.random.fold_in(own, position), (blocks,), jnp.float32, smallest / len(shards), largest / len(shards)))
        factor_of = factor_of * jnp.repeat(heights, shape[position] // blocks).reshape([-1 if axis == position else 1 for axis in range(len(shape))])
    return factor_of


def rank_table(number_of, slope):
    weights = [(1 << 20) // math.isqrt(standing ** slope) + 1 for standing in range(1, number_of + 1)]
    scale = 1 + sum(weights) // (1 << 30)
    return np.cumsum(np.array([max(1, weight // scale) for weight in weights]))


def skewed_ids(stream_key, dims, amount, slope):
    listing = rank_table(amount, slope)
    pick = jax.random.randint(jax.random.fold_in(stream_key, 1), dims, 0, int(listing[amount - 1]))
    standing = jnp.searchsorted(jnp.asarray(listing, jnp.int32), pick, side="right")
    return jax.random.permutation(jax.random.fold_in(stream_key, 2), amount)[standing].astype(jnp.int32)


def centred(own_key, dims, spread, bound, cuts=(), dtype=jnp.bfloat16):
    values = spread * jax.random.normal(own_key, dims, jnp.float32)
    if cuts:
        values = values * shard_levels(own_key, dims, cuts, -0.22, 0.18)
    return jnp.clip(values, -bound, bound).astype(dtype)


def setup_inputs(seed: int = 0) -> dict:
    splits = jax.random.split(jax.random.key(seed), 5)
    return {
        "walkers": centred(splits[0], (W, M, 4 * NOCC), 1.0, 6.0, ((0, 8), (1, 4))),
        "inverse": centred(splits[1], (W, 2, 2, NOCC, NOCC), 0.125, 0.75, ((0, 8),)),
        "vectors": centred(splits[2], (NCHOL, M, 4 * NOCC), (M * 4 * NOCC) ** -0.5, 0.015625, ((0, 8), (1, 4))),
        "sources": set_ends(skewed_ids(splits[3], (W,), W, 2), jax.random.fold_in(splits[3], 3), 0, W - 1).astype(jnp.int32),
    }


def block_of(part):
    real_part, imag_part = part[:, 0], part[:, 1]
    first = jnp.stack([real_part, imag_part], 3)
    second = jnp.stack([-imag_part, real_part], 3)
    return jnp.stack([first, second], 2)


def green(moved, moved_inverse):
    count, orbitals = moved.shape[0], moved.shape[1]
    operator = block_of(moved_inverse).astype(jnp.float32)
    parts = moved.reshape(count, orbitals, 2, 2, -1).astype(jnp.float32)
    theta = jnp.einsum('wpcsk,wsckdi->wpdsi', parts, operator, precision=lax.Precision.HIGHEST)
    return theta.reshape(count, orbitals, -1).astype(jnp.bfloat16)


def rows_of(theta):
    count, orbitals = theta.shape[0], theta.shape[1]
    split = theta.reshape(count, orbitals, 2, -1)
    first = jnp.stack([split[:, :, 0], -split[:, :, 1]], 2).reshape(count, -1)
    second = jnp.stack([split[:, :, 1], split[:, :, 0]], 2).reshape(count, -1)
    return jnp.stack([first, second], 0)


def reference(walkers, inverse, vectors, sources):
    moved = jnp.take(walkers, sources, axis=0)
    moved_inverse = jnp.take(inverse, sources, axis=0)
    theta = green(moved, moved_inverse)
    stacked = rows_of(theta).reshape(2 * W, -1)
    block = math.gcd(NCHOL, 1024)
    blocks = vectors.reshape(NCHOL // block, block, -1)

    def one_block(piece):
        return lax.dot_general(stacked, piece, (((1,), (1,)), ((), ())), preferred_element_type=jnp.float32)

    result = lax.map(one_block, blocks)
    result = jnp.moveaxis(result, 0, 1).reshape(2, W, NCHOL)
    return moved, result
```

```python
import functools

import jax
import jax.numpy as jnp
from jax import lax
from jax.experimental import pallas as pl
from jax.experimental.pallas import tpu as pltpu
from jax.sharding import PartitionSpec as P

VMEM_LIMIT = 66_000_000


def divisor_of(size, choices):
    for choice in choices:
        if size % choice == 0:
            return choice
    return size


def operator_of(packed_inverse):
    plain = packed_inverse.astype(jnp.float32)
    lane = lax.broadcasted_iota(jnp.int32, plain.shape, 1)
    half = plain.shape[1] // 2
    quarter = half // 2
    swapped = jnp.concatenate([-plain[:, half:], plain[:, :half]], 1)
    up = (lane // quarter) % 2 == 0
    theta = jnp.concatenate(
        [
            jnp.where(up, plain, 0.0),
            jnp.where(up, 0.0, plain),
            jnp.where(up, swapped, 0.0),
            jnp.where(up, 0.0, swapped),
        ],
        0,
    )
    first = jnp.concatenate([theta[:, :half], -theta[:, half:]], 1)
    second = jnp.concatenate([theta[:, half:], theta[:, :half]], 1)
    return jnp.concatenate([first, second], 1).astype(jnp.bfloat16)


def theta_kernel(local_count, scalars, *refs):
    walker_refs, inverse_refs = refs[:local_count], refs[local_count : 2 * local_count]
    rows_ref, moved_ref, first_ref, second_ref = refs[2 * local_count :]
    for j in range(local_count):
        operator = operator_of(inverse_refs[j][0])
        both = jnp.dot(walker_refs[j][0], operator, preferred_element_type=jnp.float32)
        both = both.astype(jnp.bfloat16)
        width = both.shape[1] // 2
        first_ref[j] = both[:, :width]
        second_ref[j] = both[:, width:]

    @pl.when(pl.program_id(0) == scalars[0])
    def _():
        for j in range(local_count):
            moved_ref[j] = walker_refs[j][0]

    rows_ref[:, 0] = jnp.swapaxes(first_ref[...], 0, 1)
    rows_ref[:, 1] = jnp.swapaxes(second_ref[...], 0, 1)


def theta_rows(walkers, inverses, inverse_at, scalars, local_count, orbitals, occupied):
    width = walkers.shape[2]
    count = scalars.shape[0] - 1

    def spec(j, height, at):
        return pl.BlockSpec((1, height, width), lambda b, s: (s[1 + b * local_count + j], at, 0))

    each = range(local_count)
    return pl.pallas_call(
        functools.partial(theta_kernel, local_count),
        out_shape=(
            jax.ShapeDtypeStruct((orbitals, 2, count, width), jnp.bfloat16),
            jax.ShapeDtypeStruct((local_count, orbitals, width), jnp.bfloat16),
        ),
        grid_spec=pltpu.PrefetchScalarGridSpec(
            num_scalar_prefetch=1,
            grid=(count // local_count,),
            in_specs=[spec(j, orbitals, 0) for j in each]
            + [spec(j, occupied, inverse_at // occupied) for j in each],
            out_specs=(
                pl.BlockSpec((orbitals, 2, local_count, width), lambda b, s: (0, 0, b, 0)),
                pl.BlockSpec((local_count, orbitals, width), lambda b, s: (0, 0, 0)),
            ),
            scratch_shapes=[pltpu.VMEM((local_count, orbitals, width), jnp.bfloat16)] * 2,
        ),
        cost_estimate=pl.CostEstimate(
            flops=16 * count * orbitals * width * width,
            bytes_accessed=6 * count * orbitals * width,
            transcendentals=0,
        ),
        compiler_params=pltpu.CompilerParams(vmem_limit_bytes=VMEM_LIMIT),
        name="theta_rows",
    )(scalars, *([walkers] * local_count), *([inverses] * local_count))


def bias_kernel(group, rows_ref, vectors_ref, *refs):
    out_ref = refs[-1]
    depth = pl.program_id(1)
    chunk = vectors_ref.shape[1]

    @pl.when(depth == 0)
    def _():
        out_ref[...] = refs[0][...] if len(refs) > 1 else jnp.zeros_like(out_ref)

    for at in range(0, chunk, group):
        turned = jnp.swapaxes(vectors_ref[:, at : at + group, :], 0, 1)
        right = jnp.concatenate([turned[q] for q in range(group)], 1)
        held = rows_ref[pl.ds(depth * chunk + at, group)]
        left = jnp.concatenate([held[q] for q in range(group)], 1)
        out_ref[...] += lax.dot_general(
            left, right, (((1,), (1,)), ((), ())), preferred_element_type=jnp.float32
        )


def bias_terms(rows, vectors, begin, chunk, *before):
    orbitals, height, width = rows.shape
    count = vectors.shape[0]
    tile = divisor_of(count, (256, 128))
    out_spec = pl.BlockSpec((height, tile), lambda g, k: (0, g))
    return pl.pallas_call(
        functools.partial(bias_kernel, divisor_of(chunk, (16,))),
        out_shape=jax.ShapeDtypeStruct((height, count), jnp.float32),
        grid=(count // tile, orbitals // chunk),
        in_specs=[
            pl.BlockSpec((orbitals, height, width), lambda g, k: (0, 0, 0), pipeline_mode=pl.Buffered(1)),
            pl.BlockSpec((tile, chunk, width), lambda g, k: (g, k + begin // chunk, 0)),
        ]
        + [out_spec] * len(before),
        out_specs=out_spec,
        cost_estimate=pl.CostEstimate(
            flops=4 * orbitals * height * width * count,
            bytes_accessed=2 * orbitals * width * (count + height),
            transcendentals=0,
        ),
        compiler_params=pltpu.CompilerParams(vmem_limit_bytes=VMEM_LIMIT),
        name="bias_terms",
    )(rows, vectors, *before)


def per_device(walkers, inverse, vectors, sources):
    local_count, orbitals, width = walkers.shape
    occupied = inverse.shape[-1]
    count = sources.shape[0]
    split = -(-5 * orbitals // (8 * occupied)) * occupied
    small = jnp.transpose(inverse, (0, 3, 1, 2, 4)).reshape(local_count, occupied, width)
    early = jnp.concatenate([walkers[:, :split], small], 1)
    early = lax.all_gather(early, "walk", axis=0, tiled=True)
    late = lax.all_gather(walkers[:, split:], "walk", axis=0, tiled=True)
    scalars = jnp.concatenate([lax.axis_index("walk")[None].astype(jnp.int32), sources])
    rows, moved_early = theta_rows(early, early, split, scalars, local_count, split, occupied)
    bias = bias_terms(rows.reshape(split, 2 * count, width), vectors, 0, occupied)
    rest = orbitals - split
    rows, moved_late = theta_rows(late, early, split, scalars, local_count, rest, occupied)
    bias = bias_terms(rows.reshape(rest, 2 * count, width), vectors, split, occupied, bias)
    moved = jnp.concatenate([moved_early, moved_late], 1)
    force_bias = lax.psum_scatter(
        bias.reshape(2, count, -1), "vec", scatter_dimension=1, tiled=True
    )
    return (moved, force_bias)


def solution(mesh):
    in_specs = (
        P("walk", "vec", None),
        P("walk", None, None, None, None),
        P("walk", "vec", None),
        P(),
    )
    out_specs = (P("walk", "vec", None), P(None, "vec", "walk"))
    return jax.shard_map(
        per_device, mesh=mesh, in_specs=in_specs, out_specs=out_specs, check_vma=False
    )
```
